32 devices in a mesh: gx: 8 (over y, x, core), gy: 4 (over z).
Axes of the slice: x: 2, y: 2, z: 4, core: 2. Of those that a mesh axis runs over, the one named last changes fastest.
Arguments:
- elevation: float32 [8, 128, 1024], P(None, 'gy', 'gx'), may hold values from -4 to 4
- east_velocity: float32 [8, 128, 1024], P(None, 'gy', 'gx'), may hold values from -3 to 3
- north_velocity: float32 [8, 128, 1024], P(None, 'gy', 'gx'), may hold values from -3 to 3
- water_depth: float32 [128, 1024], P('gy', 'gx'), may hold values from 0.3 to 1
- land_sea: int32 [128, 1024], P('gy', 'gx'), may hold values 0 or 1
Outputs:
- surface: float32 [8, 128, 1024], P(None, 'gy', 'gx')
- east_flow: float32 [8, 128, 1024], P(None, 'gy', 'gx')
- north_flow: float32 [8, 128, 1024], P(None, 'gy', 'gx')
- loading: float32 [8, 16, 128], P(None, 'gy', 'gx')
The draws below stay inside these ranges and needn't reach their ends.
All inputs are finite; a program needn't handle non-finite values. No bound on the sum of `land_sea` on one device may be relied on, other than what follows from the above.
Results may differ from the reference program's by a relative error of at most 0.0032.
Values may be sent and summed in bfloat16 or wider, within the bound.
A program may use at most 64 MiB of HBM per device.

```python
import math
import jax
import jax.numpy as jnp
from jax import lax

MEMBERS = 8
STEPS = 4
INTERVALS = 2
BLOCK = 8
NX = 1024
NY = 128


def draw_elevation(key, part):
    full_shape = (MEMBERS, NY, NX)
    return jnp.clip(jax.random.normal(jax.random.fold_in(key, 12), full_shape, jnp.float32), -4.0, 4.0)


def place_ends(result, key, smallest, top_value):
    extent = result.shape
    place = [jax.random.randint(jax.random.fold_in(key, axis), (), 0, extent[axis]) for axis in range(len(extent))]
    result = result.at[tuple(place)].set(smallest)
    longest = extent.index(max(extent))
    place[longest] = (place[longest] + 1) % extent[longest]
    return result.at[tuple(place)].set(top_value)


def levels(own_key, dims, split, smallest, top_value):
    gain = 1.0
    for axis_at, blocks in split:
        steps = jax.random.uniform(jax.random.fold_in(jax.random.fold_in(own_key, 6), axis_at), (blocks,), jnp.float32, smallest / len(split), top_value / len(split))
        gain = gain * jnp.repeat(jnp.exp(steps), dims[axis_at] // blocks).reshape((-1,) + (1,) * (len(dims) - 1 - axis_at))
    return gain


def noise(stream_key, extent, width, limit, pieces=(), held_as=jnp.bfloat16):
    drawn = width * jax.random.normal(stream_key, extent, jnp.float32)
    if pieces:
        drawn = drawn * levels(stream_key, extent, pieces, -0.22, 0.18)
    return jnp.clip(drawn, -limit, limit).astype(held_as)


def setup_inputs(seed: int = 0) -> dict:
    splits = jax.random.split(jax.random.key(seed), 6)
    elevation = draw_elevation(jax.random.fold_in(splits[5], 71), 0)
    east_velocity = noise(splits[1], (MEMBERS, NY, NX), 0.5, 3.0, ((1, 4), (2, 8)), jnp.float32)
    north_velocity = noise(splits[2], (MEMBERS, NY, NX), 0.5, 3.0, ((1, 4), (2, 8)), jnp.float32)
    water_depth = jnp.clip(0.3 + 0.7 * jax.random.uniform(splits[3], (NY, NX), jnp.float32) ** levels(splits[3], (NY, NX), ((0, 4), (1, 8)), -0.2, 0.2), 0.3, 1.0)
    land_sea = place_ends((jax.random.randint(splits[4], (NY, NX), 0, 10) < 7).astype(jnp.int32), jax.random.fold_in(splits[4], 1), 0, 1)
    return dict(elevation=elevation, east_velocity=east_velocity, north_velocity=north_velocity, water_depth=water_depth, land_sea=land_sea)


COURANT = 0.35
FRICTION = 0.02
CORIOLIS = 0.3
GREEN_SCALE = 0.25

def latitude(row_ids, row_count):
    return ((row_ids.astype(jnp.float32) + 0.5) / row_count - 0.5) * jnp.pi

def longitude(col_ids, col_count):
    return (col_ids.astype(jnp.float32) + 0.5) / col_count * (2.0 * jnp.pi)

def unit_vectors(lat_angle, lon_angle):
    return (jnp.cos(lat_angle) * jnp.cos(lon_angle), jnp.cos(lat_angle) * jnp.sin(lon_angle), jnp.sin(lat_angle))

def green_block(source, target, coarse_rows):
    first = source[0][:, None] - target[0][None, :]
    second = source[1][:, None] - target[1][None, :]
    third = source[2][:, None] - target[2][None, :]
    chord_len = jnp.sqrt(first * first + second * second + third * third)
    return (GREEN_SCALE / (1.0 + chord_len * (coarse_rows / math.pi))).astype(jnp.bfloat16)

def coarse_loads(height, ocean):
    members, row_total, col_total = height.shape
    blocks = (ocean * height).reshape(members, row_total // BLOCK, BLOCK, col_total // BLOCK, BLOCK)
    return (lax.optimization_barrier(jnp.sum(blocks, axis=(2, 4))) / BLOCK).astype(jnp.bfloat16)

def refine(loading):
    members, row_blocks, col_blocks = loading.shape
    spread = jnp.broadcast_to(loading[:, :, None, :, None], (members, row_blocks, BLOCK, col_blocks, BLOCK))
    return spread.reshape(members, row_blocks * BLOCK, col_blocks * BLOCK)

def velocities(padded, east_now, north_now, ocean, turning):
    grad_east = (padded[:, 1:-1, 2:] - padded[:, 1:-1, :-2]) * 0.5
    grad_north = (padded[:, 2:, 1:-1] - padded[:, :-2, 1:-1]) * 0.5
    east_next = ocean * (east_now + turning * north_now - COURANT * grad_east - FRICTION * east_now)
    north_next = ocean * (north_now - turning * east_now - COURANT * grad_north - FRICTION * north_now)
    return (east_next, north_next)

def surface_update(height, east_rim, north_rim, ocean):
    outflow = (east_rim[:, :, 2:] - east_rim[:, :, :-2]) * 0.5 + (north_rim[:, 2:, :] - north_rim[:, :-2, :]) * 0.5
    return height - ocean * COURANT * outflow

def wrap_east(field):
    return jnp.concatenate([field[:, :, -1:], field, field[:, :, :1]], axis=2)

def zero_north(field):
    return jnp.pad(field, ((0, 0), (1, 1), (0, 0)))

def reference(elevation, east_velocity, north_velocity, water_depth, land_sea):
    ocean = land_sea.astype(jnp.float32)
    row_blocks = NY // BLOCK
    col_blocks = NX // BLOCK
    turning = (CORIOLIS * jnp.sin(latitude(jnp.arange(NY, dtype=jnp.int32), NY)))[:, None]
    block_rows = jnp.arange(row_blocks, dtype=jnp.int32)
    block_cols = jnp.arange(col_blocks, dtype=jnp.int32)
    source = unit_vectors(latitude(jnp.repeat(block_rows, col_blocks), row_blocks), longitude(jnp.tile(block_cols, row_blocks), col_blocks))
    target_lon = longitude(block_cols, col_blocks)
    height, east_now, north_now = (elevation, east_velocity, north_velocity)
    loading = jnp.zeros((MEMBERS, row_blocks, col_blocks), jnp.float32)
    for interval in range(INTERVALS):
        block_loads = coarse_loads(height, ocean).reshape(MEMBERS, row_blocks * col_blocks).astype(jnp.float32)

        def target_row(row_index):
            row_ids = jnp.zeros((col_blocks,), jnp.int32) + row_index
            target = unit_vectors(latitude(row_ids, row_blocks), target_lon)
            green = green_block(source, target, row_blocks).astype(jnp.float32)
            return jnp.dot(block_loads, green, precision=lax.Precision.HIGHEST)
        loading = jnp.transpose(lax.map(target_row, block_rows), (1, 0, 2))
        fine_sal = refine(loading)
        for substep in range(STEPS):
            effective = zero_north(wrap_east(height - fine_sal))
            east_next, north_next = velocities(effective, east_now, north_now, ocean, turning)
            east_rim = wrap_east(water_depth * east_next)
            north_rim = zero_north(water_depth * north_next)
            height = surface_update(height, east_rim, north_rim, ocean)
            east_now, north_now = (east_next, north_next)
    return (height, east_now, north_now, loading)
```

```python
import functools
import math

import jax
import jax.numpy as jnp
from jax import lax
from jax.experimental import pallas as pl
from jax.experimental.pallas import tpu as pltpu
from jax.sharding import PartitionSpec as P

STEPS = 4
INTERVALS = 2
BLOCK = 8
HALO = 2 * STEPS

COURANT = 0.35
FRICTION = 0.02
CORIOLIS = 0.3
GREEN_SCALE = 0.25
CHUNK = 8

MESH = pl.DeviceIdType.MESH
F32 = jnp.float32
BF16 = jnp.bfloat16
DIRS = ((0, 1), (0, -1), (1, 0), (-1, 0), (1, 1), (1, -1), (-1, 1), (-1, -1))


def iota(shape, dim):
    return lax.broadcasted_iota(jnp.int32, shape, dim)


def latitude(row_ids, row_count):
    return ((row_ids.astype(F32) + 0.5) / row_count - 0.5) * jnp.pi


def longitude(col_ids, col_count):
    return (col_ids.astype(F32) + 0.5) / col_count * (2.0 * jnp.pi)


def unit_vectors(lat_angle, lon_angle):
    cos_lat = jnp.cos(lat_angle)
    return (cos_lat * jnp.cos(lon_angle), cos_lat * jnp.sin(lon_angle), jnp.sin(lat_angle))


def split3(x):
    hi = x.astype(BF16).astype(F32)
    rest = x - hi
    mid = rest.astype(BF16).astype(F32)
    return jnp.concatenate([hi, mid, rest - mid], axis=0).astype(BF16)


def exact_dot(x, table):
    rows = x.shape[0]
    out = jnp.dot(split3(x), table, preferred_element_type=F32)
    return out[:rows] + out[rows : 2 * rows] + out[2 * rows :]


def kernel(
    nx, ny, members, rows, cols,
    h_in, u_in, v_in, d_in, o_in,
    h_out, u_out, v_out, l_out,
    in3, in_d, in_o, own, strips, land, slab, st, st_land, st_ns, dmx, turn,
    eta, uu, vv, green, tiles, fine, ind, expand,
    in_sem, gs_sem, gr_sem, hs_sem, hr_sem, ss_sem, sr_sem,
):
    gx, gy = lax.axis_index("gx"), lax.axis_index("gy")
    n = nx * ny
    rb_own, cb_own = rows // BLOCK, cols // BLOCK
    per_device = rb_own * cb_own
    pair_rows = 2 * per_device
    coarse_rows, coarse_cols = rb_own * ny, cb_own * nx
    ext = rows + 2 * HALO
    ext_tiles = ext // BLOCK
    my_slot = ((gx // 2) * ny + gy) * 2 + gx % 2
    lane = iota((members, cols), 1)

    inputs = [
        pltpu.make_async_copy(src, dst, in_sem.at[k])
        for k, (src, dst) in enumerate(
            ((h_in, in3.at[0]), (u_in, in3.at[1]), (v_in, in3.at[2]), (d_in, in_d), (o_in, in_o))
        )
    ]
    for copy in inputs:
        copy.start()

    def partner(offset):
        slot = lax.rem(my_slot + offset, n)
        pair = slot // 2
        return {"gx": (pair // ny) * 2 + slot % 2, "gy": pair % ny}

    barrier = pltpu.get_barrier_semaphore()

    def greet(offset, carry):
        pl.semaphore_signal(barrier, inc=1, device_id=partner(offset), device_id_type=MESH)
        return carry

    lax.fori_loop(1, n, greet, 0)

    def target_of(dx, dy):
        return {"gx": lax.rem(gx + dx + nx, nx), "gy": gy + dy}

    def when(dy, sending, fn):
        if dy == 0:
            fn()
        else:
            beyond = gy + (dy if sending else -dy)
            pl.when((beyond >= 0) & (beyond < ny))(fn)

    def static_copy(k):
        dx, dy = DIRS[k]
        side = 0 if dx > 0 else 1
        if dy == 0:
            src, dst = st, st_land.at[side, pl.ds(HALO, rows)]
        else:
            src = st.at[pl.ds(rows - HALO if dy > 0 else 0, HALO)]
            at = 0 if dy > 0 else HALO + rows
            dst = st_ns.at[0 if dy > 0 else 1] if dx == 0 else st_land.at[side, pl.ds(at, HALO)]
        return pltpu.make_async_remote_copy(
            src_ref=src, dst_ref=dst, send_sem=ss_sem.at[k], recv_sem=sr_sem.at[k],
            device_id=target_of(dx, dy), device_id_type=MESH,
        )

    def halo_copy(i, k):
        dx, dy = DIRS[k]
        side = 0 if dx > 0 else 1
        if dx == 0:
            src = own.at[:, pl.ds(rows - HALO if dy > 0 else 0, HALO)]
            dst = slab.at[i, 0 if dy > 0 else 1]
        elif dy == 0:
            src, dst = strips.at[i], land.at[i, side, :, pl.ds(1, rb_own)]
        else:
            src = strips.at[i, :, pl.ds(rb_own - 1 if dy > 0 else 0, 1)]
            dst = land.at[i, side, :, pl.ds(0 if dy > 0 else ext_tiles - 1, 1)]
        return pltpu.make_async_remote_copy(
            src_ref=src, dst_ref=dst, send_sem=hs_sem.at[i, k], recv_sem=hr_sem.at[i, k],
            device_id=target_of(dx, dy), device_id_type=MESH,
        )

    def clear(side):
        at = 0 if side == 0 else ext_tiles - 1
        slab[:, side] = jnp.zeros_like(slab[:, side])
        land[:, :, :, at] = jnp.zeros_like(land[:, :, :, at])
        st_ns[side] = jnp.zeros_like(st_ns[side])
        st_land[:, at * BLOCK : (at + 1) * BLOCK] = jnp.zeros((2, HALO, cols), F32)

    pl.when(gy == 0)(lambda: clear(0))
    pl.when(gy == ny - 1)(lambda: clear(1))

    k_id = iota((rb_own * cols, pair_rows), 0)
    lane_id = iota((rb_own * cols, pair_rows), 1)
    wanted = (gx % 2) * per_device + (k_id // cols) * cb_own + (k_id % cols) // BLOCK
    ind[...] = jnp.where(wanted == lane_id, 1.0, 0.0).astype(BF16)

    for copy in inputs:
        copy.wait()
    st[...] = jnp.where(in_o[...] > 0, in_d[...], 0.0)
    for k in range(rows):
        for f in range(3):
            own[f, k] = in3[f, pl.ds(k, members, stride=rows), :]

    pl.semaphore_wait(barrier, n - 1)
    for k, (dx, dy) in enumerate(DIRS):
        when(dy, True, lambda k=k: static_copy(k).start())

    def setup():
        t = iota((8, 128), 1)
        north = per_device
        south = north + cb_own
        west = south + cb_own
        east = west + rb_own + 2
        t_row = jnp.where(t < north, t // cb_own, jnp.where(t < south, -1, rb_own))
        t_col = jnp.where(t < north, t % cb_own, jnp.where(t < south, t - north, t - south))
        t_row = jnp.where(t >= east, t - east - 1, jnp.where(t >= west, t - west - 1, t_row))
        t_col = jnp.where(t >= east, cb_own, jnp.where(t >= west, -1, t_col))
        t_row = gy * rb_own + t_row
        t_col = gx * cb_own + t_col
        t_col = jnp.where(t_col < 0, t_col + coarse_cols, t_col)
        t_col = jnp.where(t_col >= coarse_cols, t_col - coarse_cols, t_col)
        target = unit_vectors(latitude(t_row, coarse_rows), longitude(t_col, coarse_cols))
        target = [jnp.broadcast_to(x[:1], (pair_rows, 128)) for x in target]

        def green_group(g, carry):
            p = g * 8 + iota((8, pair_rows), 0)
            k = iota((8, pair_rows), 1)
            s_col = ((p // ny) * 2 + k // per_device) * cb_own + k % cb_own
            s_row = (p % ny) * rb_own + (k % per_device) // cb_own
            source = unit_vectors(latitude(s_row, coarse_rows), longitude(s_col, coarse_cols))
            source = [jnp.transpose(x) for x in source]
            for j in range(8):
                square = None
                for s, t_vec in zip(source, target):
                    diff = jnp.broadcast_to(s[:, j : j + 1], (pair_rows, 128)) - t_vec
                    square = diff * diff if square is None else square + diff * diff
                value = GREEN_SCALE / (1.0 + jnp.sqrt(square) * (coarse_rows / math.pi))
                green[g * 8 + j] = value.astype(BF16)
            return carry

        lax.fori_loop(0, n // 16, green_group, 0)

        t_id = iota((128, 2 * cols), 0)
        l_id = iota((128, 2 * cols), 1)
        for e in range(ext_tiles):
            base = north if e == 0 else south if e == ext_tiles - 1 else (e - 1) * cb_own
            want = jnp.where(
                l_id < cols, base + l_id // BLOCK, jnp.where(l_id < cols + cols // 2, east + e, west + e)
            )
            expand[:, e * 2 * cols : (e + 1) * 2 * cols] = jnp.where(want == t_id, 1.0, 0.0).astype(BF16)

        for e in range(ext_tiles):
            row_ids = gy * rows - HALO + e * BLOCK + iota((BLOCK, cols), 0)
            turning = CORIOLIS * jnp.sin(latitude(row_ids, rows * ny))
            for k in range(BLOCK):
                turn[e * BLOCK + k] = jnp.broadcast_to(turning[k : k + 1], (members, cols))

        for k, (dx, dy) in enumerate(DIRS):
            when(dy, False, lambda k=k: static_copy(k).wait_recv())
            when(dy, True, lambda k=k: static_copy(k).wait_send())
        for e in range(ext_tiles):
            if e == 0:
                main = st_ns[0]
            elif e == ext_tiles - 1:
                main = st_ns[1]
            else:
                main = st[(e - 1) * BLOCK : e * BLOCK]
            part = slice(e * BLOCK, (e + 1) * BLOCK)
            side = jnp.where(iota((BLOCK, cols), 1) < cols // 2, st_land[1, part], st_land[0, part])
            for k in range(BLOCK):
                dmx[e * BLOCK + k, :, :cols] = jnp.broadcast_to(main[k : k + 1], (members, cols))
                dmx[e * BLOCK + k, :, cols:] = jnp.broadcast_to(side[k : k + 1], (members, cols))

    def xdiff(m, a):
        rm, ra = pltpu.roll(m, cols - 1, 1), pltpu.roll(a, cols - 1, 1)
        lm, la = pltpu.roll(m, 1, 1), pltpu.roll(a, 1, 1)
        at_end, at_start = lane == cols - 1, lane == 0
        return (
            jnp.where(at_end, ra, rm) - jnp.where(at_start, la, lm),
            jnp.where(at_end, rm, ra) - jnp.where(at_start, lm, la),
        )

    half = 0.5 * COURANT
    keep = 1.0 - FRICTION

    def sweep(step):
        src, dst = step % 2, 1 - step % 2
        start, count = 1 + 2 * step, ext - 2 - 4 * step

        def pair(ref, r):
            return ref[r, :, :cols], ref[r, :, cols:]

        def one_row(r, carry):
            before, here, north_two, north_one, flow_one = carry
            after = pair(eta.at[src], r + 1)
            u_now, v_now = pair(uu.at[src], r), pair(vv.at[src], r)
            depth, depth_one = pair(dmx, r), pair(dmx, r - 1)
            coriolis = turn[r]
            grad = xdiff(*here)
            du, dv = [], []
            for c in range(2):
                part = slice(c * cols, (c + 1) * cols)
                wet = depth[c] > 0.0
                u_next = keep * u_now[c] + coriolis * v_now[c] - half * grad[c]
                v_next = keep * v_now[c] - coriolis * u_now[c] - half * (after[c] - before[c])
                u_next = jnp.where(wet, u_next, 0.0)
                v_next = jnp.where(wet, v_next, 0.0)
                uu[dst, r, :, part] = u_next
                vv[dst, r, :, part] = v_next
                du.append(depth[c] * u_next)
                dv.append(depth[c] * v_next)
            flow = xdiff(*du)
            for c in range(2):
                part = slice(c * cols, (c + 1) * cols)
                out = half * (flow_one[c] + (dv[c] - north_two[c]))
                eta[dst, r - 1, :, part] = jnp.where(depth_one[c] > 0.0, before[c] - out, before[c])
            return here, after, north_one, tuple(dv), flow

        def chunk(first, amount, carry):
            for k in range(amount):
                carry = one_row(first + k, carry)
            return carry

        zero = jnp.zeros((members, cols), F32)
        zeros = (zero, zero)
        carry = (pair(eta.at[src], start - 1), pair(eta.at[src], start), zeros, zeros, zeros)
        full = count // CHUNK
        carry = lax.fori_loop(0, full, lambda c, x: chunk(start + c * CHUNK, CHUNK, x), carry)
        chunk(start + full * CHUNK, count - full * CHUNK, carry)

    def interval(i, _):
        sums = []
        for b in range(rb_own):
            total = None
            for k in range(BLOCK):
                r = b * BLOCK + k
                mask = jnp.broadcast_to(st[r : r + 1], (members, cols)) > 0.0
                value = jnp.where(mask, own[0, r], 0.0)
                total = value if total is None else total + value
            sums.append(total)
        loads = exact_dot(jnp.concatenate(sums, axis=1), ind[...]) / BLOCK
        tiles[i, my_slot] = loads.astype(BF16)

        def gather_copy(offset):
            return pltpu.make_async_remote_copy(
                src_ref=tiles.at[i, my_slot], dst_ref=tiles.at[i, my_slot],
                send_sem=gs_sem.at[i], recv_sem=gr_sem.at[i],
                device_id=partner(offset), device_id_type=MESH,
            )

        def send(offset, carry):
            gather_copy(offset).start()
            return carry

        lax.fori_loop(1, n, send, 0)
        for k in (0, 1):
            when(DIRS[k][1], True, lambda k=k: halo_copy(i, k).start())

        for f in range(3):
            for b in range(rb_own):
                packed = None
                for k in range(BLOCK):
                    moved = pltpu.roll(own[f, b * BLOCK + k], (HALO + 2 * HALO * k) % cols, 1)
                    packed = moved if packed is None else jnp.where(lane // (2 * HALO) == k, moved, packed)
                strips[i, f, b] = packed
        for k in range(2, len(DIRS)):
            when(DIRS[k][1], True, lambda k=k: halo_copy(i, k).start())

        pl.when(i == 0)(setup)

        everyone = pltpu.make_async_remote_copy(
            src_ref=tiles.at[i, pl.ds(0, n - 1)], dst_ref=tiles.at[i, pl.ds(0, n - 1)],
            send_sem=gs_sem.at[i], recv_sem=gr_sem.at[i],
            device_id=partner(1), device_id_type=MESH,
        )
        everyone.wait_recv()

        group = 16 if n // 2 % 16 == 0 else 1

        def add_group(g, total):
            for j in range(group):
                p = g * group + j
                tile = tiles[i, 2 * p].astype(F32) + tiles[i, 2 * p + 1].astype(F32)
                total = total + jnp.dot(tile.astype(BF16), green[p], preferred_element_type=F32)
            return total

        loading = lax.fori_loop(0, n // 2 // group, add_group, jnp.zeros((members, 128), F32))
        l_out[...] = loading[:, :per_device]
        spread = exact_dot(loading, expand[...])
        for e in range(ext_tiles):
            value = spread[:, e * 2 * cols : (e + 1) * 2 * cols]
            if e == 0:
                value = jnp.where(gy == 0, 0.0, value)
            if e == ext_tiles - 1:
                value = jnp.where(gy == ny - 1, 0.0, value)
            fine[e] = value

        for k, (dx, dy) in enumerate(DIRS):
            when(dy, False, lambda k=k: halo_copy(i, k).wait_recv())
        everyone.wait_send()
        for k, (dx, dy) in enumerate(DIRS):
            when(dy, True, lambda k=k: halo_copy(i, k).wait_send())

        for f, ref in enumerate((eta, uu, vv)):
            for e in range(ext_tiles):
                joined = jnp.where(lane % (2 * HALO) < HALO, land[i, 0, f, e], land[i, 1, f, e])
                for k in range(BLOCK):
                    r = e * BLOCK + k
                    if e == 0:
                        main = slab[i, 0, f, k]
                    elif e == ext_tiles - 1:
                        main = slab[i, 1, f, k]
                    else:
                        main = own[f, r - HALO]
                    side = pltpu.roll(joined, (-(2 * HALO * k + HALO)) % cols, 1)
                    if f == 0:
                        main = main - fine[e, :, :cols]
                        side = side - fine[e, :, cols:]
                    ref[0, r, :, :cols] = main
                    ref[0, r, :, cols:] = side

        for step in range(STEPS):
            sweep(step)
        last = STEPS % 2
        for r in range(rows):
            own[0, r] = eta[last, HALO + r, :, :cols] + fine[1 + r // BLOCK, :, :cols]
            own[1, r] = uu[last, HALO + r, :, :cols]
            own[2, r] = vv[last, HALO + r, :, :cols]
        return 0

    lax.fori_loop(0, INTERVALS, interval, 0)
    for r in range(rows):
        for f, out in enumerate((h_out, u_out, v_out)):
            out[pl.ds(r, members, stride=rows), :] = own[f, r]


def shards(nx, ny, elevation, east_velocity, north_velocity, water_depth, land_sea):
    members, rows, cols = elevation.shape
    rb_own, cb_own = rows // BLOCK, cols // BLOCK
    n = nx * ny
    ext = rows + 2 * HALO
    tiles = ext // BLOCK
    flat = (members * rows, cols)
    any_spec = pl.BlockSpec(memory_space=pl.ANY)
    vmem_spec = pl.BlockSpec(memory_space=pltpu.VMEM)
    dma = pltpu.SemaphoreType.DMA
    field = jax.ShapeDtypeStruct(flat, F32)
    h, u, v, loading = pl.pallas_call(
        functools.partial(kernel, nx, ny, members, rows, cols),
        out_shape=(field, field, field, jax.ShapeDtypeStruct((members, rb_own * cb_own), F32)),
        in_specs=[any_spec] * 5,
        out_specs=(vmem_spec,) * 4,
        scratch_shapes=[
            pltpu.VMEM((3,) + flat, F32),
            pltpu.VMEM((rows, cols), F32),
            pltpu.VMEM((rows, cols), jnp.int32),
            pltpu.VMEM((3, rows, members, cols), F32),
            pltpu.VMEM((INTERVALS, 3, rb_own, members, cols), F32),
            pltpu.VMEM((INTERVALS, 2, 3, tiles, members, cols), F32),
            pltpu.VMEM((INTERVALS, 2, 3, HALO, members, cols), F32),
            pltpu.VMEM((rows, cols), F32),
            pltpu.VMEM((2, ext, cols), F32),
            pltpu.VMEM((2, HALO, cols), F32),
            pltpu.VMEM((ext, members, 2 * cols), F32),
            pltpu.VMEM((ext, members, cols), F32),
            pltpu.VMEM((2, ext, members, 2 * cols), F32),
            pltpu.VMEM((2, ext, members, 2 * cols), F32),
            pltpu.VMEM((2, ext, members, 2 * cols), F32),
            pltpu.VMEM((n // 2, 2 * rb_own * cb_own, 128), BF16),
            pltpu.VMEM((INTERVALS, n, members, 2 * rb_own * cb_own), BF16),
            pltpu.VMEM((tiles, members, 2 * cols), F32),
            pltpu.VMEM((rb_own * cols, 2 * rb_own * cb_own), BF16),
            pltpu.VMEM((128, tiles * 2 * cols), BF16),
            dma((5,)),
            dma((INTERVALS,)),
            dma((INTERVALS,)),
            dma((INTERVALS, len(DIRS))),
            dma((INTERVALS, len(DIRS))),
            dma((len(DIRS),)),
            dma((len(DIRS),)),
        ],
        compiler_params=pltpu.CompilerParams(
            collective_id=0, has_side_effects=True, vmem_limit_bytes=48 * 1024 * 1024
        ),
        name="tide",
    )(
        elevation.reshape(flat), east_velocity.reshape(flat), north_velocity.reshape(flat),
        water_depth, land_sea,
    )
    shape = (members, rows, cols)
    return (h.reshape(shape), u.reshape(shape), v.reshape(shape), loading.reshape(members, rb_own, cb_own))


def solution(mesh):
    nx, ny = mesh.shape["gx"], mesh.shape["gy"]
    tile = P(None, "gy", "gx")
    return jax.shard_map(
        functools.partial(shards, nx, ny),
        mesh=mesh,
        in_specs=(tile, tile, tile, P("gy", "gx"), P("gy", "gx")),
        out_specs=(tile, tile, tile, tile),
        check_vma=False,
    )
```

```python
import functools
import math

import jax
import jax.numpy as jnp
from jax import lax
from jax.experimental import pallas as pl
from jax.experimental.pallas import tpu as pltpu
from jax.sharding import PartitionSpec as P

STEPS = 4
INTERVALS = 2
BLOCK = 8
HALO = 2 * STEPS

COURANT = 0.35
FRICTION = 0.02
CORIOLIS = 0.3
GREEN_SCALE = 0.25
CHUNK = 8

MESH = pl.DeviceIdType.MESH
F32 = jnp.float32
BF16 = jnp.bfloat16
DIRS = ((0, 1), (0, -1), (1, 0), (-1, 0), (1, 1), (1, -1), (-1, 1), (-1, -1))


def iota(shape, dim):
    return lax.broadcasted_iota(jnp.int32, shape, dim)


def latitude(row_ids, row_count):
    return ((row_ids.astype(F32) + 0.5) / row_count - 0.5) * jnp.pi


def longitude(col_ids, col_count):
    return (col_ids.astype(F32) + 0.5) / col_count * (2.0 * jnp.pi)


def unit_vectors(lat_angle, lon_angle):
    cos_lat = jnp.cos(lat_angle)
    return (cos_lat * jnp.cos(lon_angle), cos_lat * jnp.sin(lon_angle), jnp.sin(lat_angle))


def split3(x):
    hi = x.astype(BF16).astype(F32)
    rest = x - hi
    mid = rest.astype(BF16).astype(F32)
    return jnp.concatenate([hi, mid, rest - mid], axis=0).astype(BF16)


def exact_dot(x, table):
    rows = x.shape[0]
    out = jnp.dot(split3(x), table, preferred_element_type=F32)
    return out[:rows] + out[rows : 2 * rows] + out[2 * rows :]


def kernel(
    nx, ny, members, rows, cols,
    h_in, u_in, v_in, d_in, o_in,
    own, l_out,
    in3, in_d, in_o, strips, land, slab, st, st_land, st_ns, dmx, turn,
    eta, uu, vv, green, tiles, fine, ind, expand,
    in_sem, gs_sem, gr_sem, hs_sem, hr_sem, ss_sem, sr_sem,
):
    gx, gy = lax.axis_index("gx"), lax.axis_index("gy")
    n = nx * ny
    rb_own, cb_own = rows // BLOCK, cols // BLOCK
    per_device = rb_own * cb_own
    pair_rows = 2 * per_device
    coarse_rows, coarse_cols = rb_own * ny, cb_own * nx
    ext = rows + 2 * HALO
    ext_tiles = ext // BLOCK
    my_slot = ((gx // 2) * ny + gy) * 2 + gx % 2
    lane = iota((members, cols), 1)

    inputs = [
        pltpu.make_async_copy(src, dst, in_sem.at[k])
        for k, (src, dst) in enumerate(
            ((h_in, in3.at[0]), (u_in, in3.at[1]), (v_in, in3.at[2]), (d_in, in_d), (o_in, in_o))
        )
    ]
    for copy in inputs:
        copy.start()

    def wrap(index, size):
        return jnp.where(index >= size, index - size, index)

    def to_all_others(fn):
        others = [wrap(gy + dy, ny) for dy in range(ny)]
        for y in others[1:]:
            fn({"gx": gx, "gy": y})

        def column(dx, carry):
            x = wrap(gx + dx, nx)
            for y in others:
                fn({"gx": x, "gy": y})
            return carry

        lax.fori_loop(1, nx, column, 0)

    barrier = pltpu.get_barrier_semaphore()

    to_all_others(
        lambda device: pl.semaphore_signal(barrier, inc=1, device_id=device, device_id_type=MESH)
    )

    def target_of(dx, dy):
        return {"gx": wrap(jnp.where(gx + dx < 0, gx + dx + nx, gx + dx), nx), "gy": gy + dy}

    def when(dy, sending, fn):
        if dy == 0:
            fn()
        else:
            beyond = gy + (dy if sending else -dy)
            pl.when((beyond >= 0) & (beyond < ny))(fn)

    def static_copy(k):
        dx, dy = DIRS[k]
        side = 0 if dx > 0 else 1
        if dy == 0:
            src, dst = st, st_land.at[side, pl.ds(HALO, rows)]
        else:
            src = st.at[pl.ds(rows - HALO if dy > 0 else 0, HALO)]
            at = 0 if dy > 0 else HALO + rows
            dst = st_ns.at[0 if dy > 0 else 1] if dx == 0 else st_land.at[side, pl.ds(at, HALO)]
        return pltpu.make_async_remote_copy(
            src_ref=src, dst_ref=dst, send_sem=ss_sem.at[k], recv_sem=sr_sem.at[k],
            device_id=target_of(dx, dy), device_id_type=MESH,
        )

    def halo_copy(i, k):
        dx, dy = DIRS[k]
        side = 0 if dx > 0 else 1
        if dx == 0:
            src = own.at[:, pl.ds(rows - HALO if dy > 0 else 0, HALO)]
            dst = slab.at[i, 0 if dy > 0 else 1]
        elif dy == 0:
            src, dst = strips.at[i], land.at[i, side, :, pl.ds(1, rb_own)]
        else:
            src = strips.at[i, :, pl.ds(rb_own - 1 if dy > 0 else 0, 1)]
            dst = land.at[i, side, :, pl.ds(0 if dy > 0 else ext_tiles - 1, 1)]
        return pltpu.make_async_remote_copy(
            src_ref=src, dst_ref=dst, send_sem=hs_sem.at[i, k], recv_sem=hr_sem.at[i, k],
            device_id=target_of(dx, dy), device_id_type=MESH,
        )

    def clear(side):
        at = 0 if side == 0 else ext_tiles - 1
        slab[:, side] = jnp.zeros_like(slab[:, side])
        land[:, :, :, at] = jnp.zeros_like(land[:, :, :, at])
        st_ns[side] = jnp.zeros_like(st_ns[side])
        st_land[:, at * BLOCK : (at + 1) * BLOCK] = jnp.zeros((2, HALO, cols), F32)

    pl.when(gy == 0)(lambda: clear(0))
    pl.when(gy == ny - 1)(lambda: clear(1))

    k_id = iota((rb_own * cols, pair_rows), 0)
    lane_id = iota((rb_own * cols, pair_rows), 1)
    wanted = (gx % 2) * per_device + (k_id // cols) * cb_own + (k_id % cols) // BLOCK
    ind[...] = jnp.where(wanted == lane_id, 1.0, 0.0).astype(BF16)

    for copy in inputs:
        copy.wait()
    st[...] = jnp.where(in_o[...] > 0, in_d[...], 0.0)
    for k in range(rows):
        for f in range(3):
            own[f, k] = in3[f, pl.ds(k, members, stride=rows), :]

    def early_setup():
        north = per_device
        south = north + cb_own
        west = south + cb_own
        east = west + rb_own + 2
        t_id = iota((128, 2 * cols), 0)
        l_id = iota((128, 2 * cols), 1)
        for e in range(ext_tiles):
            base = north if e == 0 else south if e == ext_tiles - 1 else (e - 1) * cb_own
            want = jnp.where(
                l_id < cols, base + l_id // BLOCK, jnp.where(l_id < cols + cols // 2, east + e, west + e)
            )
            expand[:, e * 2 * cols : (e + 1) * 2 * cols] = jnp.where(want == t_id, 1.0, 0.0).astype(BF16)

        for e in range(ext_tiles):
            row_ids = gy * rows - HALO + e * BLOCK + iota((BLOCK, cols), 0)
            turning = CORIOLIS * jnp.sin(latitude(row_ids, rows * ny))
            for k in range(BLOCK):
                turn[e * BLOCK + k] = jnp.broadcast_to(turning[k : k + 1], (members, cols))

    def setup():
        t = iota((8, 128), 1)
        north = per_device
        south = north + cb_own
        west = south + cb_own
        east = west + rb_own + 2
        t_row = jnp.where(t < north, t // cb_own, jnp.where(t < south, -1, rb_own))
        t_col = jnp.where(t < north, t % cb_own, jnp.where(t < south, t - north, t - south))
        t_row = jnp.where(t >= east, t - east - 1, jnp.where(t >= west, t - west - 1, t_row))
        t_col = jnp.where(t >= east, cb_own, jnp.where(t >= west, -1, t_col))
        t_row = gy * rb_own + t_row
        t_col = gx * cb_own + t_col
        t_col = jnp.where(t_col < 0, t_col + coarse_cols, t_col)
        t_col = jnp.where(t_col >= coarse_cols, t_col - coarse_cols, t_col)
        target = unit_vectors(latitude(t_row, coarse_rows), longitude(t_col, coarse_cols))
        target = [jnp.broadcast_to(x[:1], (pair_rows, 128)) for x in target]

        def green_group(g, carry):
            p = g * 8 + iota((8, pair_rows), 0)
            k = iota((8, pair_rows), 1)
            s_col = ((p // ny) * 2 + k // per_device) * cb_own + k % cb_own
            s_row = (p % ny) * rb_own + (k % per_device) // cb_own
            source = unit_vectors(latitude(s_row, coarse_rows), longitude(s_col, coarse_cols))
            source = [jnp.transpose(x) for x in source]
            for j in range(8):
                square = None
                for s, t_vec in zip(source, target):
                    diff = jnp.broadcast_to(s[:, j : j + 1], (pair_rows, 128)) - t_vec
                    square = diff * diff if square is None else square + diff * diff
                value = GREEN_SCALE / (1.0 + jnp.sqrt(square) * (coarse_rows / math.pi))
                green[g * 8 + j] = value.astype(BF16)
            return carry

        lax.fori_loop(0, n // 16, green_group, 0)

        for k, (dx, dy) in enumerate(DIRS):
            when(dy, False, lambda k=k: static_copy(k).wait_recv())
            when(dy, True, lambda k=k: static_copy(k).wait_send())
        for e in range(ext_tiles):
            if e == 0:
                main = st_ns[0]
            elif e == ext_tiles - 1:
                main = st_ns[1]
            else:
                main = st[(e - 1) * BLOCK : e * BLOCK]
            part = slice(e * BLOCK, (e + 1) * BLOCK)
            side = jnp.where(iota((BLOCK, cols), 1) < cols // 2, st_land[1, part], st_land[0, part])
            for k in range(BLOCK):
                dmx[e * BLOCK + k, :, :cols] = jnp.broadcast_to(main[k : k + 1], (members, cols))
                dmx[e * BLOCK + k, :, cols:] = jnp.broadcast_to(side[k : k + 1], (members, cols))

    def xdiff(m, a):
        rm, ra = pltpu.roll(m, cols - 1, 1), pltpu.roll(a, cols - 1, 1)
        lm, la = pltpu.roll(m, 1, 1), pltpu.roll(a, 1, 1)
        at_end, at_start = lane == cols - 1, lane == 0
        return (
            jnp.where(at_end, ra, rm) - jnp.where(at_start, la, lm),
            jnp.where(at_end, rm, ra) - jnp.where(at_start, lm, la),
        )

    half = 0.5 * COURANT
    keep = 1.0 - FRICTION

    def sweep(step):
        src, dst = step % 2, 1 - step % 2
        start, count = 1 + 2 * step, ext - 2 - 4 * step

        def pair(ref, r):
            return ref[r, :, :cols], ref[r, :, cols:]

        def one_row(r, carry):
            before, here, north_two, north_one, flow_one = carry
            after = pair(eta.at[src], r + 1)
            u_now, v_now = pair(uu.at[src], r), pair(vv.at[src], r)
            depth, depth_one = pair(dmx, r), pair(dmx, r - 1)
            coriolis = turn[r]
            grad = xdiff(*here)
            du, dv = [], []
            for c in range(2):
                part = slice(c * cols, (c + 1) * cols)
                wet = depth[c] > 0.0
                u_next = keep * u_now[c] + coriolis * v_now[c] - half * grad[c]
                v_next = keep * v_now[c] - coriolis * u_now[c] - half * (after[c] - before[c])
                u_next = jnp.where(wet, u_next, 0.0)
                v_next = jnp.where(wet, v_next, 0.0)
                uu[dst, r, :, part] = u_next
                vv[dst, r, :, part] = v_next
                du.append(depth[c] * u_next)
                dv.append(depth[c] * v_next)
            flow = xdiff(*du)
            for c in range(2):
                part = slice(c * cols, (c + 1) * cols)
                out = half * (flow_one[c] + (dv[c] - north_two[c]))
                eta[dst, r - 1, :, part] = jnp.where(depth_one[c] > 0.0, before[c] - out, before[c])
            return here, after, north_one, tuple(dv), flow

        def chunk(first, amount, carry):
            for k in range(amount):
                carry = one_row(first + k, carry)
            return carry

        zero = jnp.zeros((members, cols), F32)
        zeros = (zero, zero)
        carry = (pair(eta.at[src], start - 1), pair(eta.at[src], start), zeros, zeros, zeros)
        full = count // CHUNK
        carry = lax.fori_loop(0, full, lambda c, x: chunk(start + c * CHUNK, CHUNK, x), carry)
        chunk(start + full * CHUNK, count - full * CHUNK, carry)

    def begin(i):
        sums = []
        for b in range(rb_own):
            total = None
            for k in range(BLOCK):
                r = b * BLOCK + k
                mask = jnp.broadcast_to(st[r : r + 1], (members, cols)) > 0.0
                value = jnp.where(mask, own[0, r], 0.0)
                total = value if total is None else total + value
            sums.append(total)
        loads = exact_dot(jnp.concatenate(sums, axis=1), ind[...]) / BLOCK
        tiles[i, my_slot] = loads.astype(BF16)

        for f in range(3):
            for b in range(rb_own):
                packed = None
                for k in range(BLOCK):
                    moved = pltpu.roll(own[f, b * BLOCK + k], (HALO + 2 * HALO * k) % cols, 1)
                    packed = moved if packed is None else jnp.where(lane // (2 * HALO) == k, moved, packed)
                strips[i, f, b] = packed

    def interval(i, _):
        def send(device):
            pltpu.make_async_remote_copy(
                src_ref=tiles.at[i, my_slot], dst_ref=tiles.at[i, my_slot],
                send_sem=gs_sem.at[i], recv_sem=gr_sem.at[i],
                device_id=device, device_id_type=MESH,
            ).start()

        to_all_others(send)
        for k in range(len(DIRS)):
            when(DIRS[k][1], True, lambda k=k: halo_copy(i, k).start())

        pl.when(i == 0)(setup)

        everyone = pltpu.make_async_remote_copy(
            src_ref=tiles.at[i, pl.ds(0, n - 1)], dst_ref=tiles.at[i, pl.ds(0, n - 1)],
            send_sem=gs_sem.at[i], recv_sem=gr_sem.at[i],
            device_id=target_of(1, 0), device_id_type=MESH,
        )
        everyone.wait_recv()

        group = 16 if n // 2 % 16 == 0 else 1

        def add_group(g, total):
            for j in range(group):
                p = g * group + j
                tile = tiles[i, 2 * p].astype(F32) + tiles[i, 2 * p + 1].astype(F32)
                total = total + jnp.dot(tile.astype(BF16), green[p], preferred_element_type=F32)
            return total

        loading = lax.fori_loop(0, n // 2 // group, add_group, jnp.zeros((members, 128), F32))
        l_out[...] = loading[:, :per_device]
        spread = exact_dot(loading, expand[...])
        for e in range(ext_tiles):
            value = spread[:, e * 2 * cols : (e + 1) * 2 * cols]
            if e == 0:
                value = jnp.where(gy == 0, 0.0, value)
            if e == ext_tiles - 1:
                value = jnp.where(gy == ny - 1, 0.0, value)
            fine[e] = value

        for k, (dx, dy) in enumerate(DIRS):
            when(dy, False, lambda k=k: halo_copy(i, k).wait_recv())
        everyone.wait_send()
        for k, (dx, dy) in enumerate(DIRS):
            when(dy, True, lambda k=k: halo_copy(i, k).wait_send())

        for f, ref in enumerate((eta, uu, vv)):
            for e in range(ext_tiles):
                joined = jnp.where(lane % (2 * HALO) < HALO, land[i, 0, f, e], land[i, 1, f, e])
                for k in range(BLOCK):
                    r = e * BLOCK + k
                    if e == 0:
                        main = slab[i, 0, f, k]
                    elif e == ext_tiles - 1:
                        main = slab[i, 1, f, k]
                    else:
                        main = own[f, r - HALO]
                    side = pltpu.roll(joined, (-(2 * HALO * k + HALO)) % cols, 1)
                    if f == 0:
                        main = main - fine[e, :, :cols]
                        side = side - fine[e, :, cols:]
                    ref[0, r, :, :cols] = main
                    ref[0, r, :, cols:] = side

        for step in range(STEPS):
            sweep(step)
        last = STEPS % 2
        for r in range(rows):
            own[0, r] = eta[last, HALO + r, :, :cols] + fine[1 + r // BLOCK, :, :cols]
            own[1, r] = uu[last, HALO + r, :, :cols]
            own[2, r] = vv[last, HALO + r, :, :cols]
        pl.when(i < INTERVALS - 1)(lambda: begin(i + 1))
        return 0

    begin(0)
    early_setup()
    pl.semaphore_wait(barrier, n - 1)
    for k, (dx, dy) in enumerate(DIRS):
        when(dy, True, lambda k=k: static_copy(k).start())
    lax.fori_loop(0, INTERVALS, interval, 0)


def place_outputs(members, rows, own, l_in, h_out, u_out, v_out, l_out, staged, l_staged, sem):
    copies = [
        pltpu.make_async_copy(staged.at[f], out, sem.at[f]) for f, out in enumerate((h_out, u_out, v_out))
    ]
    for f in range(3):
        for r in range(rows):
            staged[f, pl.ds(r, members, stride=rows), :] = own[f, r]
        copies[f].start()
    blocks, width = l_staged.shape[1:]
    for b in range(blocks):
        l_staged[:, b, :] = l_in[:, b * width : (b + 1) * width]
    copies.append(pltpu.make_async_copy(l_staged, l_out, sem.at[3]))
    copies[3].start()
    for copy in copies:
        copy.wait()


def shards(nx, ny, elevation, east_velocity, north_velocity, water_depth, land_sea):
    members, rows, cols = elevation.shape
    rb_own, cb_own = rows // BLOCK, cols // BLOCK
    n = nx * ny
    ext = rows + 2 * HALO
    tiles = ext // BLOCK
    flat = (members * rows, cols)
    hbm_spec = pl.BlockSpec(memory_space=pltpu.HBM)
    vmem_spec = pl.BlockSpec(memory_space=pltpu.VMEM)
    dma = pltpu.SemaphoreType.DMA
    field = jax.ShapeDtypeStruct(flat, F32)
    own, loading = pl.pallas_call(
        functools.partial(kernel, nx, ny, members, rows, cols),
        out_shape=(
            jax.ShapeDtypeStruct((3, rows, members, cols), F32),
            jax.ShapeDtypeStruct((members, rb_own * cb_own), F32),
        ),
        in_specs=[hbm_spec] * 5,
        out_specs=(vmem_spec,) * 2,
        scratch_shapes=[
            pltpu.VMEM((3,) + flat, F32),
            pltpu.VMEM((rows, cols), F32),
            pltpu.VMEM((rows, cols), jnp.int32),
            pltpu.VMEM((INTERVALS, 3, rb_own, members, cols), F32),
            pltpu.VMEM((INTERVALS, 2, 3, tiles, members, cols), F32),
            pltpu.VMEM((INTERVALS, 2, 3, HALO, members, cols), F32),
            pltpu.VMEM((rows, cols), F32),
            pltpu.VMEM((2, ext, cols), F32),
            pltpu.VMEM((2, HALO, cols), F32),
            pltpu.VMEM((ext, members, 2 * cols), F32),
            pltpu.VMEM((ext, members, cols), F32),
            pltpu.VMEM((2, ext, members, 2 * cols), F32),
            pltpu.VMEM((2, ext, members, 2 * cols), F32),
            pltpu.VMEM((2, ext, members, 2 * cols), F32),
            pltpu.VMEM((n // 2, 2 * rb_own * cb_own, 128), BF16),
            pltpu.VMEM((INTERVALS, n, members, 2 * rb_own * cb_own), BF16),
            pltpu.VMEM((tiles, members, 2 * cols), F32),
            pltpu.VMEM((rb_own * cols, 2 * rb_own * cb_own), BF16),
            pltpu.VMEM((128, tiles * 2 * cols), BF16),
            dma((5,)),
            dma((INTERVALS,)),
            dma((INTERVALS,)),
            dma((INTERVALS, len(DIRS))),
            dma((INTERVALS, len(DIRS))),
            dma((len(DIRS),)),
            dma((len(DIRS),)),
        ],
        compiler_params=pltpu.CompilerParams(
            collective_id=0, has_side_effects=True, vmem_limit_bytes=48 * 1024 * 1024
        ),
        name="tide",
    )(
        *(
            pltpu.with_memory_space_constraint(x, pltpu.HBM)
            for x in (
                elevation.reshape(flat), east_velocity.reshape(flat), north_velocity.reshape(flat),
                water_depth, land_sea,
            )
        )
    )
    coarse = jax.ShapeDtypeStruct((members, rb_own, cb_own), F32)
    h, u, v, loading = pl.pallas_call(
        functools.partial(place_outputs, members, rows),
        out_shape=(field, field, field, coarse),
        in_specs=[vmem_spec] * 2,
        out_specs=(hbm_spec,) * 4,
        scratch_shapes=[pltpu.VMEM((3,) + flat, F32), pltpu.VMEM(coarse.shape, F32), dma((4,))],
        compiler_params=pltpu.CompilerParams(vmem_limit_bytes=4 * 1024 * 1024),
        name="place",
    )(own, loading)
    shape = (members, rows, cols)
    return (h.reshape(shape), u.reshape(shape), v.reshape(shape), loading)


def solution(mesh):
    nx, ny = mesh.shape["gx"], mesh.shape["gy"]
    tile = P(None, "gy", "gx")
    return jax.shard_map(
        functools.partial(shards, nx, ny),
        mesh=mesh,
        in_specs=(tile, tile, tile, P("gy", "gx"), P("gy", "gx")),
        out_specs=(tile, tile, tile, tile),
        check_vma=False,
    )
```

```python
import functools
import math

import jax
import jax.numpy as jnp
from jax import lax
from jax.experimental import pallas as pl
from jax.experimental.pallas import tpu as pltpu
from jax.sharding import PartitionSpec as P

STEPS = 4
INTERVALS = 2
BLOCK = 8
HALO = 2 * STEPS

COURANT = 0.35
FRICTION = 0.02
CORIOLIS = 0.3
GREEN_SCALE = 0.25
CHUNK = 8

MESH = pl.DeviceIdType.MESH
F32 = jnp.float32
BF16 = jnp.bfloat16
DIRS = ((0, 1), (0, -1), (1, 0), (-1, 0), (1, 1), (1, -1), (-1, 1), (-1, -1))


def iota(shape, dim):
    return lax.broadcasted_iota(jnp.int32, shape, dim)


def latitude(row_ids, row_count):
    return ((row_ids.astype(F32) + 0.5) / row_count - 0.5) * jnp.pi


def longitude(col_ids, col_count):
    return (col_ids.astype(F32) + 0.5) / col_count * (2.0 * jnp.pi)


def unit_vectors(lat_angle, lon_angle):
    cos_lat = jnp.cos(lat_angle)
    return (cos_lat * jnp.cos(lon_angle), cos_lat * jnp.sin(lon_angle), jnp.sin(lat_angle))


def split3(x):
    hi = x.astype(BF16).astype(F32)
    rest = x - hi
    mid = rest.astype(BF16).astype(F32)
    return jnp.concatenate([hi, mid, rest - mid], axis=0).astype(BF16)


def exact_dot(x, table):
    rows = x.shape[0]
    out = jnp.dot(split3(x), table, preferred_element_type=F32)
    return out[:rows] + out[rows : 2 * rows] + out[2 * rows :]


def kernel(
    nx, ny, members, rows, cols,
    h_in, u_in, v_in, d_in, o_in,
    own, l_out,
    in3, in_d, in_o, strips, land, slab, st, st_land, st_ns, dmx, turn,
    eta, uu, vv, green, tiles, fine, ind, expand,
    in_sem, gs_sem, gr_sem, hs_sem, hr_sem, ss_sem, sr_sem,
):
    gx, gy = lax.axis_index("gx"), lax.axis_index("gy")
    n = nx * ny
    rb_own, cb_own = rows // BLOCK, cols // BLOCK
    per_device = rb_own * cb_own
    pair_rows = 2 * per_device
    coarse_rows, coarse_cols = rb_own * ny, cb_own * nx
    ext = rows + 2 * HALO
    ext_tiles = ext // BLOCK
    my_slot = ((gx // 2) * ny + gy) * 2 + gx % 2
    lane = iota((members, cols), 1)
    half = 0.5 * COURANT

    inputs = [
        pltpu.make_async_copy(src, dst, in_sem.at[k])
        for k, (src, dst) in enumerate(
            ((h_in, in3.at[0]), (u_in, in3.at[1]), (v_in, in3.at[2]), (d_in, in_d), (o_in, in_o))
        )
    ]
    for copy in inputs:
        copy.start()

    def wrap(index, size):
        return jnp.where(index >= size, index - size, index)

    def to_all_others(fn):
        others = [wrap(gy + dy, ny) for dy in range(ny)]
        for y in others[1:]:
            fn({"gx": gx, "gy": y})

        def column(dx, carry):
            x = wrap(gx + dx, nx)
            for y in others:
                fn({"gx": x, "gy": y})
            return carry

        lax.fori_loop(1, nx, column, 0)

    barrier = pltpu.get_barrier_semaphore()

    to_all_others(
        lambda device: pl.semaphore_signal(barrier, inc=1, device_id=device, device_id_type=MESH)
    )

    def target_of(dx, dy):
        return {"gx": wrap(jnp.where(gx + dx < 0, gx + dx + nx, gx + dx), nx), "gy": gy + dy}

    def when(dy, sending, fn):
        if dy == 0:
            fn()
        else:
            beyond = gy + (dy if sending else -dy)
            pl.when((beyond >= 0) & (beyond < ny))(fn)

    def static_copy(k):
        dx, dy = DIRS[k]
        side = 0 if dx > 0 else 1
        if dy == 0:
            src, dst = st, st_land.at[side, pl.ds(HALO, rows)]
        else:
            src = st.at[pl.ds(rows - HALO if dy > 0 else 0, HALO)]
            at = 0 if dy > 0 else HALO + rows
            dst = st_ns.at[0 if dy > 0 else 1] if dx == 0 else st_land.at[side, pl.ds(at, HALO)]
        return pltpu.make_async_remote_copy(
            src_ref=src, dst_ref=dst, send_sem=ss_sem.at[k], recv_sem=sr_sem.at[k],
            device_id=target_of(dx, dy), device_id_type=MESH,
        )

    def halo_copy(i, k):
        dx, dy = DIRS[k]
        side = 0 if dx > 0 else 1
        if dx == 0:
            src = own.at[:, pl.ds(rows - HALO if dy > 0 else 0, HALO)]
            dst = slab.at[i, 0 if dy > 0 else 1]
        elif dy == 0:
            src, dst = strips.at[i], land.at[i, side, :, pl.ds(1, rb_own)]
        else:
            src = strips.at[i, :, pl.ds(rb_own - 1 if dy > 0 else 0, 1)]
            dst = land.at[i, side, :, pl.ds(0 if dy > 0 else ext_tiles - 1, 1)]
        return pltpu.make_async_remote_copy(
            src_ref=src, dst_ref=dst, send_sem=hs_sem.at[i, k], recv_sem=hr_sem.at[i, k],
            device_id=target_of(dx, dy), device_id_type=MESH,
        )

    def clear(side):
        at = 0 if side == 0 else ext_tiles - 1
        slab[:, side] = jnp.zeros_like(slab[:, side])
        land[:, :, :, at] = jnp.zeros_like(land[:, :, :, at])
        st_ns[side] = jnp.zeros_like(st_ns[side])
        st_land[:, at * BLOCK : (at + 1) * BLOCK] = jnp.zeros((2, HALO, cols), F32)

    pl.when(gy == 0)(lambda: clear(0))
    pl.when(gy == ny - 1)(lambda: clear(1))

    k_id = iota((rb_own * cols, pair_rows), 0)
    lane_id = iota((rb_own * cols, pair_rows), 1)
    wanted = (gx % 2) * per_device + (k_id // cols) * cb_own + (k_id % cols) // BLOCK
    ind[...] = jnp.where(wanted == lane_id, 1.0, 0.0).astype(BF16)

    for copy in inputs:
        copy.wait()
    st[...] = jnp.where(in_o[...] > 0, in_d[...], 0.0)
    for k in range(rows):
        for f in range(3):
            own[f, k] = in3[f, pl.ds(k, members, stride=rows), :]

    def early_setup():
        north = per_device
        south = north + cb_own
        west = south + cb_own
        east = west + rb_own + 2
        t_id = iota((128, 2 * cols), 0)
        l_id = iota((128, 2 * cols), 1)
        for e in range(ext_tiles):
            base = north if e == 0 else south if e == ext_tiles - 1 else (e - 1) * cb_own
            want = jnp.where(
                l_id < cols, base + l_id // BLOCK, jnp.where(l_id < cols + cols // 2, east + e, west + e)
            )
            expand[:, e * 2 * cols : (e + 1) * 2 * cols] = jnp.where(want == t_id, 1.0, 0.0).astype(BF16)

        for e in range(ext_tiles):
            row_ids = gy * rows - HALO + e * BLOCK + iota((BLOCK, cols), 0)
            turning = CORIOLIS * jnp.sin(latitude(row_ids, rows * ny))
            for k in range(BLOCK):
                turn[e * BLOCK + k] = jnp.broadcast_to(turning[k : k + 1], (members, cols))

    def setup():
        t = iota((8, 128), 1)
        north = per_device
        south = north + cb_own
        west = south + cb_own
        east = west + rb_own + 2
        t_row = jnp.where(t < north, t // cb_own, jnp.where(t < south, -1, rb_own))
        t_col = jnp.where(t < north, t % cb_own, jnp.where(t < south, t - north, t - south))
        t_row = jnp.where(t >= east, t - east - 1, jnp.where(t >= west, t - west - 1, t_row))
        t_col = jnp.where(t >= east, cb_own, jnp.where(t >= west, -1, t_col))
        t_row = gy * rb_own + t_row
        t_col = gx * cb_own + t_col
        t_col = jnp.where(t_col < 0, t_col + coarse_cols, t_col)
        t_col = jnp.where(t_col >= coarse_cols, t_col - coarse_cols, t_col)
        target = unit_vectors(latitude(t_row, coarse_rows), longitude(t_col, coarse_cols))
        target = [jnp.broadcast_to(x[:1], (pair_rows, 128)) for x in target]

        def green_group(g, carry):
            p = g * 8 + iota((8, pair_rows), 0)
            k = iota((8, pair_rows), 1)
            s_col = ((p // ny) * 2 + k // per_device) * cb_own + k % cb_own
            s_row = (p % ny) * rb_own + (k % per_device) // cb_own
            source = unit_vectors(latitude(s_row, coarse_rows), longitude(s_col, coarse_cols))
            source = [jnp.transpose(x) for x in source]
            for j in range(8):
                square = None
                for s, t_vec in zip(source, target):
                    diff = jnp.broadcast_to(s[:, j : j + 1], (pair_rows, 128)) - t_vec
                    square = diff * diff if square is None else square + diff * diff
                value = GREEN_SCALE / (1.0 + jnp.sqrt(square) * (coarse_rows / math.pi))
                green[g * 8 + j] = value.astype(BF16)
            return carry

        lax.fori_loop(0, n // 16, green_group, 0)

        for k, (dx, dy) in enumerate(DIRS):
            when(dy, False, lambda k=k: static_copy(k).wait_recv())
            when(dy, True, lambda k=k: static_copy(k).wait_send())
        for e in range(ext_tiles):
            if e == 0:
                main = st_ns[0]
            elif e == ext_tiles - 1:
                main = st_ns[1]
            else:
                main = st[(e - 1) * BLOCK : e * BLOCK]
            part = slice(e * BLOCK, (e + 1) * BLOCK)
            side = jnp.where(iota((BLOCK, cols), 1) < cols // 2, st_land[1, part], st_land[0, part])
            main, side = main * (half * half), side * (half * half)
            for k in range(BLOCK):
                dmx[e * BLOCK + k, :, :cols] = jnp.broadcast_to(main[k : k + 1], (members, cols))
                dmx[e * BLOCK + k, :, cols:] = jnp.broadcast_to(side[k : k + 1], (members, cols))

    def xdiff(m, a):
        rm, ra = pltpu.roll(m, cols - 1, 1), pltpu.roll(a, cols - 1, 1)
        lm, la = pltpu.roll(m, 1, 1), pltpu.roll(a, 1, 1)
        at_end, at_start = lane == cols - 1, lane == 0
        return (
            jnp.where(at_end, ra, rm) - jnp.where(at_start, la, lm),
            jnp.where(at_end, rm, ra) - jnp.where(at_start, lm, la),
        )

    keep = 1.0 - FRICTION

    def sweep(step):
        src, dst = step % 2, 1 - step % 2
        start, count = 1 + 2 * step, ext - 2 - 4 * step

        def pair(ref, r):
            return ref[r, :, :cols], ref[r, :, cols:]

        def one_row(r, carry):
            before, here, north_two, north_one, flow_one = carry
            after = pair(eta.at[src], r + 1)
            u_now, v_now = pair(uu.at[src], r), pair(vv.at[src], r)
            depth, depth_one = pair(dmx, r), pair(dmx, r - 1)
            coriolis = turn[r]
            grad = xdiff(*here)
            du, dv = [], []
            for c in range(2):
                part = slice(c * cols, (c + 1) * cols)
                wet = depth[c] > 0.0
                u_next = keep * u_now[c] + coriolis * v_now[c] - grad[c]
                v_next = keep * v_now[c] - coriolis * u_now[c] - (after[c] - before[c])
                u_next = jnp.where(wet, u_next, 0.0)
                v_next = jnp.where(wet, v_next, 0.0)
                uu[dst, r, :, part] = u_next
                vv[dst, r, :, part] = v_next
                du.append(depth[c] * u_next)
                dv.append(depth[c] * v_next)
            flow = xdiff(*du)
            for c in range(2):
                part = slice(c * cols, (c + 1) * cols)
                out = flow_one[c] + (dv[c] - north_two[c])
                eta[dst, r - 1, :, part] = jnp.where(depth_one[c] > 0.0, before[c] - out, before[c])
            return here, after, north_one, tuple(dv), flow

        def chunk(first, amount, carry):
            for k in range(amount):
                carry = one_row(first + k, carry)
            return carry

        zero = jnp.zeros((members, cols), F32)
        zeros = (zero, zero)
        carry = (pair(eta.at[src], start - 1), pair(eta.at[src], start), zeros, zeros, zeros)
        full = count // CHUNK
        carry = lax.fori_loop(0, full, lambda c, x: chunk(start + c * CHUNK, CHUNK, x), carry)
        chunk(start + full * CHUNK, count - full * CHUNK, carry)

    def begin(i):
        sums = []
        for b in range(rb_own):
            total = None
            for k in range(BLOCK):
                r = b * BLOCK + k
                mask = jnp.broadcast_to(st[r : r + 1], (members, cols)) > 0.0
                value = jnp.where(mask, own[0, r], 0.0)
                total = value if total is None else total + value
            sums.append(total)
        loads = exact_dot(jnp.concatenate(sums, axis=1), ind[...]) / BLOCK
        tiles[i, my_slot] = loads.astype(BF16)

        for f in range(3):
            for b in range(rb_own):
                packed = None
                for k in range(BLOCK):
                    moved = pltpu.roll(own[f, b * BLOCK + k], (HALO + 2 * HALO * k) % cols, 1)
                    packed = moved if packed is None else jnp.where(lane // (2 * HALO) == k, moved, packed)
                strips[i, f, b] = packed

    def interval(i, _):
        def send(device):
            pltpu.make_async_remote_copy(
                src_ref=tiles.at[i, my_slot], dst_ref=tiles.at[i, my_slot],
                send_sem=gs_sem.at[i], recv_sem=gr_sem.at[i],
                device_id=device, device_id_type=MESH,
            ).start()

        to_all_others(send)
        for k in range(len(DIRS)):
            when(DIRS[k][1], True, lambda k=k: halo_copy(i, k).start())

        for r in range(rows):
            uu[0, HALO + r, :, :cols] = own[1, r]
            vv[0, HALO + r, :, :cols] = own[2, r]

        pl.when(i == 0)(setup)

        everyone = pltpu.make_async_remote_copy(
            src_ref=tiles.at[i, pl.ds(0, n - 1)], dst_ref=tiles.at[i, pl.ds(0, n - 1)],
            send_sem=gs_sem.at[i], recv_sem=gr_sem.at[i],
            device_id=target_of(1, 0), device_id_type=MESH,
        )
        everyone.wait_recv()

        group = 16 if n // 2 % 16 == 0 else 1

        def add_group(g, total):
            for j in range(group):
                p = g * group + j
                tile = tiles[i, 2 * p].astype(F32) + tiles[i, 2 * p + 1].astype(F32)
                total = total + jnp.dot(tile.astype(BF16), green[p], preferred_element_type=F32)
            return total

        loading = lax.fori_loop(0, n // 2 // group, add_group, jnp.zeros((members, 128), F32))
        l_out[...] = loading[:, :per_device]
        spread = exact_dot(loading, expand[...])
        for e in range(ext_tiles):
            value = spread[:, e * 2 * cols : (e + 1) * 2 * cols]
            if e == 0:
                value = jnp.where(gy == 0, 0.0, value)
            if e == ext_tiles - 1:
                value = jnp.where(gy == ny - 1, 0.0, value)
            fine[e] = value

        for k, (dx, dy) in enumerate(DIRS):
            when(dy, False, lambda k=k: halo_copy(i, k).wait_recv())
        everyone.wait_send()
        for k, (dx, dy) in enumerate(DIRS):
            when(dy, True, lambda k=k: halo_copy(i, k).wait_send())

        for f, ref in enumerate((eta, uu, vv)):
            for e in range(ext_tiles):
                joined = jnp.where(lane % (2 * HALO) < HALO, land[i, 0, f, e], land[i, 1, f, e])
                for k in range(BLOCK):
                    r = e * BLOCK + k
                    if e == 0:
                        main = slab[i, 0, f, k]
                    elif e == ext_tiles - 1:
                        main = slab[i, 1, f, k]
                    else:
                        main = own[f, r - HALO]
                    side = pltpu.roll(joined, (-(2 * HALO * k + HALO)) % cols, 1)
                    if f == 0:
                        main = half * (main - fine[e, :, :cols])
                        side = half * (side - fine[e, :, cols:])
                    if f == 0 or e in (0, ext_tiles - 1):
                        ref[0, r, :, :cols] = main
                    ref[0, r, :, cols:] = side

        for step in range(STEPS):
            sweep(step)
        last = STEPS % 2
        for r in range(rows):
            own[0, r] = eta[last, HALO + r, :, :cols] * (1.0 / half) + fine[1 + r // BLOCK, :, :cols]
            own[1, r] = uu[last, HALO + r, :, :cols]
            own[2, r] = vv[last, HALO + r, :, :cols]
        pl.when(i < INTERVALS - 1)(lambda: begin(i + 1))
        return 0

    begin(0)
    early_setup()
    pl.semaphore_wait(barrier, n - 1)
    for k, (dx, dy) in enumerate(DIRS):
        when(dy, True, lambda k=k: static_copy(k).start())
    lax.fori_loop(0, INTERVALS, interval, 0)


def place_outputs(members, rows, own, l_in, h_out, u_out, v_out, l_out, staged, l_staged, sem):
    copies = [
        pltpu.make_async_copy(staged.at[f], out, sem.at[f]) for f, out in enumerate((h_out, u_out, v_out))
    ]
    for f in range(3):
        for r in range(rows):
            staged[f, pl.ds(r, members, stride=rows), :] = own[f, r]
        copies[f].start()
    blocks, width = l_staged.shape[1:]
    for b in range(blocks):
        l_staged[:, b, :] = l_in[:, b * width : (b + 1) * width]
    copies.append(pltpu.make_async_copy(l_staged, l_out, sem.at[3]))
    copies[3].start()
    for copy in copies:
        copy.wait()


def shards(nx, ny, elevation, east_velocity, north_velocity, water_depth, land_sea):
    members, rows, cols = elevation.shape
    rb_own, cb_own = rows // BLOCK, cols // BLOCK
    n = nx * ny
    ext = rows + 2 * HALO
    tiles = ext // BLOCK
    flat = (members * rows, cols)
    hbm_spec = pl.BlockSpec(memory_space=pltpu.HBM)
    vmem_spec = pl.BlockSpec(memory_space=pltpu.VMEM)
    dma = pltpu.SemaphoreType.DMA
    field = jax.ShapeDtypeStruct(flat, F32)
    own, loading = pl.pallas_call(
        functools.partial(kernel, nx, ny, members, rows, cols),
        out_shape=(
            jax.ShapeDtypeStruct((3, rows, members, cols), F32),
            jax.ShapeDtypeStruct((members, rb_own * cb_own), F32),
        ),
        in_specs=[hbm_spec] * 5,
        out_specs=(vmem_spec,) * 2,
        scratch_shapes=[
            pltpu.VMEM((3,) + flat, F32),
            pltpu.VMEM((rows, cols), F32),
            pltpu.VMEM((rows, cols), jnp.int32),
            pltpu.VMEM((INTERVALS, 3, rb_own, members, cols), F32),
            pltpu.VMEM((INTERVALS, 2, 3, tiles, members, cols), F32),
            pltpu.VMEM((INTERVALS, 2, 3, HALO, members, cols), F32),
            pltpu.VMEM((rows, cols), F32),
            pltpu.VMEM((2, ext, cols), F32),
            pltpu.VMEM((2, HALO, cols), F32),
            pltpu.VMEM((ext, members, 2 * cols), F32),
            pltpu.VMEM((ext, members, cols), F32),
            pltpu.VMEM((2, ext, members, 2 * cols), F32),
            pltpu.VMEM((2, ext, members, 2 * cols), F32),
            pltpu.VMEM((2, ext, members, 2 * cols), F32),
            pltpu.VMEM((n // 2, 2 * rb_own * cb_own, 128), BF16),
            pltpu.VMEM((INTERVALS, n, members, 2 * rb_own * cb_own), BF16),
            pltpu.VMEM((tiles, members, 2 * cols), F32),
            pltpu.VMEM((rb_own * cols, 2 * rb_own * cb_own), BF16),
            pltpu.VMEM((128, tiles * 2 * cols), BF16),
            dma((5,)),
            dma((INTERVALS,)),
            dma((INTERVALS,)),
            dma((INTERVALS, len(DIRS))),
            dma((INTERVALS, len(DIRS))),
            dma((len(DIRS),)),
            dma((len(DIRS),)),
        ],
        compiler_params=pltpu.CompilerParams(
            collective_id=0, has_side_effects=True, vmem_limit_bytes=48 * 1024 * 1024
        ),
        name="tide",
    )(
        *(
            pltpu.with_memory_space_constraint(x, pltpu.HBM)
            for x in (
                elevation.reshape(flat), east_velocity.reshape(flat), north_velocity.reshape(flat),
                water_depth, land_sea,
            )
        )
    )
    coarse = jax.ShapeDtypeStruct((members, rb_own, cb_own), F32)
    h, u, v, loading = pl.pallas_call(
        functools.partial(place_outputs, members, rows),
        out_shape=(field, field, field, coarse),
        in_specs=[vmem_spec] * 2,
        out_specs=(hbm_spec,) * 4,
        scratch_shapes=[pltpu.VMEM((3,) + flat, F32), pltpu.VMEM(coarse.shape, F32), dma((4,))],
        compiler_params=pltpu.CompilerParams(vmem_limit_bytes=4 * 1024 * 1024),
        name="place",
    )(own, loading)
    shape = (members, rows, cols)
    return (h.reshape(shape), u.reshape(shape), v.reshape(shape), loading)


def solution(mesh):
    nx, ny = mesh.shape["gx"], mesh.shape["gy"]
    tile = P(None, "gy", "gx")
    return jax.shard_map(
        functools.partial(shards, nx, ny),
        mesh=mesh,
        in_specs=(tile, tile, tile, P("gy", "gx"), P("gy", "gx")),
        out_specs=(tile, tile, tile, tile),
        check_vma=False,
    )
```

```python
import functools
import math

import jax
import jax.numpy as jnp
from jax import lax
from jax.experimental import pallas as pl
from jax.experimental.pallas import tpu as pltpu
from jax.sharding import PartitionSpec as P

STEPS = 4
INTERVALS = 2
BLOCK = 8
HALO = 2 * STEPS

COURANT = 0.35
FRICTION = 0.02
CORIOLIS = 0.3
GREEN_SCALE = 0.25
CHUNK = 8

MESH = pl.DeviceIdType.MESH
F32 = jnp.float32
BF16 = jnp.bfloat16
DIRS = ((0, 1), (0, -1), (1, 0), (-1, 0), (1, 1), (1, -1), (-1, 1), (-1, -1))


def iota(shape, dim):
    return lax.broadcasted_iota(jnp.int32, shape, dim)


def latitude(row_ids, row_count):
    return ((row_ids.astype(F32) + 0.5) / row_count - 0.5) * jnp.pi


def longitude(col_ids, col_count):
    return (col_ids.astype(F32) + 0.5) / col_count * (2.0 * jnp.pi)


def unit_vectors(lat_angle, lon_angle):
    cos_lat = jnp.cos(lat_angle)
    return (cos_lat * jnp.cos(lon_angle), cos_lat * jnp.sin(lon_angle), jnp.sin(lat_angle))


def split3(x):
    hi = x.astype(BF16).astype(F32)
    rest = x - hi
    mid = rest.astype(BF16).astype(F32)
    return jnp.concatenate([hi, mid, rest - mid], axis=0).astype(BF16)


def exact_dot(x, table):
    rows = x.shape[0]
    out = jnp.dot(split3(x), table, preferred_element_type=F32)
    return out[:rows] + out[rows : 2 * rows] + out[2 * rows :]


def kernel(
    nx, ny, members, rows, cols,
    h_in, u_in, v_in, d_in, o_in,
    own, l_out,
    in3, in_d, in_o, strips, land, slab_out, slab, st, st_land, st_ns, dmx, turn,
    eta, uu, vv, green, tiles, fine, ind, expand,
    in_sem, gs_sem, gr_sem, hs_sem, hr_sem, ss_sem, sr_sem,
):
    gx, gy = lax.axis_index("gx"), lax.axis_index("gy")
    n = nx * ny
    rb_own, cb_own = rows // BLOCK, cols // BLOCK
    per_device = rb_own * cb_own
    pair_rows = 2 * per_device
    coarse_rows, coarse_cols = rb_own * ny, cb_own * nx
    ext = rows + 2 * HALO
    ext_tiles = ext // BLOCK
    my_slot = ((gx // 2) * ny + gy) * 2 + gx % 2
    lane = iota((members, cols), 1)
    half = 0.5 * COURANT

    inputs = [
        pltpu.make_async_copy(src, dst, in_sem.at[k])
        for k, (src, dst) in enumerate(
            ((h_in, in3.at[0]), (u_in, in3.at[1]), (v_in, in3.at[2]), (d_in, in_d), (o_in, in_o))
        )
    ]
    for copy in inputs:
        copy.start()

    def wrap(index, size):
        return jnp.where(index >= size, index - size, index)

    def to_all_others(fn):
        others = [wrap(gy + dy, ny) for dy in range(ny)]
        for y in others[1:]:
            fn({"gx": gx, "gy": y})

        def column(dx, carry):
            x = wrap(gx + dx, nx)
            for y in others:
                fn({"gx": x, "gy": y})
            return carry

        lax.fori_loop(1, nx, column, 0)

    barrier = pltpu.get_barrier_semaphore()

    to_all_others(
        lambda device: pl.semaphore_signal(barrier, inc=1, device_id=device, device_id_type=MESH)
    )

    def target_of(dx, dy):
        return {"gx": wrap(jnp.where(gx + dx < 0, gx + dx + nx, gx + dx), nx), "gy": gy + dy}

    def when(dy, sending, fn):
        if dy == 0:
            fn()
        else:
            beyond = gy + (dy if sending else -dy)
            pl.when((beyond >= 0) & (beyond < ny))(fn)

    def static_copy(k):
        dx, dy = DIRS[k]
        side = 0 if dx > 0 else 1
        if dy == 0:
            src, dst = st, st_land.at[side, pl.ds(HALO, rows)]
        else:
            src = st.at[pl.ds(rows - HALO if dy > 0 else 0, HALO)]
            at = 0 if dy > 0 else HALO + rows
            dst = st_ns.at[0 if dy > 0 else 1] if dx == 0 else st_land.at[side, pl.ds(at, HALO)]
        return pltpu.make_async_remote_copy(
            src_ref=src, dst_ref=dst, send_sem=ss_sem.at[k], recv_sem=sr_sem.at[k],
            device_id=target_of(dx, dy), device_id_type=MESH,
        )

    def halo_copy(i, k):
        dx, dy = DIRS[k]
        side = 0 if dx > 0 else 1
        if dx == 0:
            at = 0 if dy > 0 else 1
            src, dst = slab_out.at[i, at], slab.at[i, at]
        elif dy == 0:
            src, dst = strips.at[i], land.at[i, side, :, pl.ds(1, rb_own)]
        else:
            src = strips.at[i, :, pl.ds(rb_own - 1 if dy > 0 else 0, 1)]
            dst = land.at[i, side, :, pl.ds(0 if dy > 0 else ext_tiles - 1, 1)]
        return pltpu.make_async_remote_copy(
            src_ref=src, dst_ref=dst, send_sem=hs_sem.at[i, k], recv_sem=hr_sem.at[i, k],
            device_id=target_of(dx, dy), device_id_type=MESH,
        )

    def clear(side):
        at = 0 if side == 0 else ext_tiles - 1
        slab[:, side] = jnp.zeros_like(slab[:, side])
        land[:, :, :, at] = jnp.zeros_like(land[:, :, :, at])
        st_ns[side] = jnp.zeros_like(st_ns[side])
        st_land[:, at * BLOCK : (at + 1) * BLOCK] = jnp.zeros((2, HALO, cols), F32)

    pl.when(gy == 0)(lambda: clear(0))
    pl.when(gy == ny - 1)(lambda: clear(1))

    k_id = iota((rb_own * cols, pair_rows), 0)
    lane_id = iota((rb_own * cols, pair_rows), 1)
    wanted = (gx % 2) * per_device + (k_id // cols) * cb_own + (k_id % cols) // BLOCK
    ind[...] = jnp.where(wanted == lane_id, 1.0, 0.0).astype(BF16)

    for copy in inputs:
        copy.wait()
    st[...] = jnp.where(in_o[...] > 0, in_d[...], 0.0)
    for k in range(rows):
        for f in range(3):
            own[f, k] = in3[f, pl.ds(k, members, stride=rows), :]

    def early_setup():
        north = per_device
        south = north + cb_own
        west = south + cb_own
        east = west + rb_own + 2
        t_id = iota((128, 2 * cols), 0)
        l_id = iota((128, 2 * cols), 1)
        for e in range(ext_tiles):
            base = north if e == 0 else south if e == ext_tiles - 1 else (e - 1) * cb_own
            want = jnp.where(
                l_id < cols, base + l_id // BLOCK, jnp.where(l_id < cols + cols // 2, east + e, west + e)
            )
            expand[:, e * 2 * cols : (e + 1) * 2 * cols] = jnp.where(want == t_id, 1.0, 0.0).astype(BF16)

        for e in range(ext_tiles):
            row_ids = gy * rows - HALO + e * BLOCK + iota((BLOCK, cols), 0)
            turning = CORIOLIS * jnp.sin(latitude(row_ids, rows * ny))
            for k in range(BLOCK):
                turn[e * BLOCK + k] = jnp.broadcast_to(turning[k : k + 1], (members, cols))

    def setup():
        t = iota((8, 128), 1)
        north = per_device
        south = north + cb_own
        west = south + cb_own
        east = west + rb_own + 2
        t_row = jnp.where(t < north, t // cb_own, jnp.where(t < south, -1, rb_own))
        t_col = jnp.where(t < north, t % cb_own, jnp.where(t < south, t - north, t - south))
        t_row = jnp.where(t >= east, t - east - 1, jnp.where(t >= west, t - west - 1, t_row))
        t_col = jnp.where(t >= east, cb_own, jnp.where(t >= west, -1, t_col))
        t_row = gy * rb_own + t_row
        t_col = gx * cb_own + t_col
        t_col = jnp.where(t_col < 0, t_col + coarse_cols, t_col)
        t_col = jnp.where(t_col >= coarse_cols, t_col - coarse_cols, t_col)
        target = unit_vectors(latitude(t_row, coarse_rows), longitude(t_col, coarse_cols))
        target = [jnp.broadcast_to(x[:1], (pair_rows, 128)) for x in target]

        def green_group(g, carry):
            p = g * 8 + iota((8, pair_rows), 0)
            k = iota((8, pair_rows), 1)
            s_col = ((p // ny) * 2 + k // per_device) * cb_own + k % cb_own
            s_row = (p % ny) * rb_own + (k % per_device) // cb_own
            source = unit_vectors(latitude(s_row, coarse_rows), longitude(s_col, coarse_cols))
            source = [jnp.transpose(x) for x in source]
            for j in range(8):
                square = None
                for s, t_vec in zip(source, target):
                    diff = jnp.broadcast_to(s[:, j : j + 1], (pair_rows, 128)) - t_vec
                    square = diff * diff if square is None else square + diff * diff
                value = GREEN_SCALE / (1.0 + jnp.sqrt(square) * (coarse_rows / math.pi))
                green[g * 8 + j] = value.astype(BF16)
            return carry

        lax.fori_loop(0, n // 16, green_group, 0)

        for k, (dx, dy) in enumerate(DIRS):
            when(dy, False, lambda k=k: static_copy(k).wait_recv())
            when(dy, True, lambda k=k: static_copy(k).wait_send())
        for e in range(ext_tiles):
            if e == 0:
                main = st_ns[0]
            elif e == ext_tiles - 1:
                main = st_ns[1]
            else:
                main = st[(e - 1) * BLOCK : e * BLOCK]
            part = slice(e * BLOCK, (e + 1) * BLOCK)
            side = jnp.where(iota((BLOCK, cols), 1) < cols // 2, st_land[1, part], st_land[0, part])
            main, side = main * (half * half), side * (half * half)
            for k in range(BLOCK):
                dmx[e * BLOCK + k, :, :cols] = jnp.broadcast_to(main[k : k + 1], (members, cols))
                dmx[e * BLOCK + k, :, cols:] = jnp.broadcast_to(side[k : k + 1], (members, cols))

    def xdiff(m, a):
        rm, ra = pltpu.roll(m, cols - 1, 1), pltpu.roll(a, cols - 1, 1)
        lm, la = pltpu.roll(m, 1, 1), pltpu.roll(a, 1, 1)
        at_end, at_start = lane == cols - 1, lane == 0
        return (
            jnp.where(at_end, ra, rm) - jnp.where(at_start, la, lm),
            jnp.where(at_end, rm, ra) - jnp.where(at_start, lm, la),
        )

    keep = 1.0 - FRICTION

    def sweep(step):
        src, dst = step % 2, 1 - step % 2
        start, count = 1 + 2 * step, ext - 2 - 4 * step

        def pair(ref, r):
            return ref[r, :, :cols], ref[r, :, cols:]

        def one_row(r, carry):
            before, here, north_two, north_one, flow_one = carry
            after = pair(eta.at[src], r + 1)
            u_now, v_now = pair(uu.at[src], r), pair(vv.at[src], r)
            depth, depth_one = pair(dmx, r), pair(dmx, r - 1)
            coriolis = turn[r]
            grad = xdiff(*here)
            du, dv = [], []
            for c in range(2):
                part = slice(c * cols, (c + 1) * cols)
                wet = depth[c] > 0.0
                u_next = keep * u_now[c] + coriolis * v_now[c] - grad[c]
                v_next = keep * v_now[c] - coriolis * u_now[c] - (after[c] - before[c])
                u_next = jnp.where(wet, u_next, 0.0)
                v_next = jnp.where(wet, v_next, 0.0)
                uu[dst, r, :, part] = u_next
                vv[dst, r, :, part] = v_next
                du.append(depth[c] * u_next)
                dv.append(depth[c] * v_next)
            flow = xdiff(*du)
            for c in range(2):
                part = slice(c * cols, (c + 1) * cols)
                out = flow_one[c] + (dv[c] - north_two[c])
                eta[dst, r - 1, :, part] = jnp.where(depth_one[c] > 0.0, before[c] - out, before[c])
            return here, after, north_one, tuple(dv), flow

        def chunk(first, amount, carry):
            for k in range(amount):
                carry = one_row(first + k, carry)
            return carry

        zero = jnp.zeros((members, cols), F32)
        zeros = (zero, zero)
        carry = (pair(eta.at[src], start - 1), pair(eta.at[src], start), zeros, zeros, zeros)
        full = count // CHUNK
        carry = lax.fori_loop(0, full, lambda c, x: chunk(start + c * CHUNK, CHUNK, x), carry)
        chunk(start + full * CHUNK, count - full * CHUNK, carry)

    def begin(i):
        sums = []
        for b in range(rb_own):
            total = None
            for k in range(BLOCK):
                r = b * BLOCK + k
                mask = jnp.broadcast_to(st[r : r + 1], (members, cols)) > 0.0
                value = jnp.where(mask, own[0, r], 0.0)
                total = value if total is None else total + value
            sums.append(total)
        loads = exact_dot(jnp.concatenate(sums, axis=1), ind[...]) / BLOCK
        tiles[i, my_slot] = loads.astype(BF16)

        for at, first in enumerate((rows - HALO, 0)):
            for f in range(3):
                for k in range(HALO // 2):
                    r = first + 2 * k
                    both = jnp.concatenate([own[f, r], own[f, r + 1]], axis=0)
                    slab_out[i, at, f, k] = both.astype(BF16)

        for f in range(3):
            for b in range(rb_own):
                packed = None
                for k in range(BLOCK):
                    moved = pltpu.roll(own[f, b * BLOCK + k], (HALO + 2 * HALO * k) % cols, 1)
                    packed = moved if packed is None else jnp.where(lane // (2 * HALO) == k, moved, packed)
                strips[i, f, b] = packed

    def interval(i, _):
        def send(device):
            pltpu.make_async_remote_copy(
                src_ref=tiles.at[i, my_slot], dst_ref=tiles.at[i, my_slot],
                send_sem=gs_sem.at[i], recv_sem=gr_sem.at[i],
                device_id=device, device_id_type=MESH,
            ).start()

        to_all_others(send)
        for k in range(len(DIRS)):
            when(DIRS[k][1], True, lambda k=k: halo_copy(i, k).start())

        for r in range(rows):
            uu[0, HALO + r, :, :cols] = own[1, r]
            vv[0, HALO + r, :, :cols] = own[2, r]

        pl.when(i == 0)(setup)

        everyone = pltpu.make_async_remote_copy(
            src_ref=tiles.at[i, pl.ds(0, n - 1)], dst_ref=tiles.at[i, pl.ds(0, n - 1)],
            send_sem=gs_sem.at[i], recv_sem=gr_sem.at[i],
            device_id=target_of(1, 0), device_id_type=MESH,
        )
        everyone.wait_recv()

        group = 16 if n // 2 % 16 == 0 else 1

        def add_group(g, total):
            for j in range(group):
                p = g * group + j
                tile = tiles[i, 2 * p].astype(F32) + tiles[i, 2 * p + 1].astype(F32)
                total = total + jnp.dot(tile.astype(BF16), green[p], preferred_element_type=F32)
            return total

        loading = lax.fori_loop(0, n // 2 // group, add_group, jnp.zeros((members, 128), F32))
        l_out[...] = loading[:, :per_device]
        spread = exact_dot(loading, expand[...])
        for e in range(ext_tiles):
            value = spread[:, e * 2 * cols : (e + 1) * 2 * cols]
            if e == 0:
                value = jnp.where(gy == 0, 0.0, value)
            if e == ext_tiles - 1:
                value = jnp.where(gy == ny - 1, 0.0, value)
            fine[e] = value

        for k, (dx, dy) in enumerate(DIRS):
            when(dy, False, lambda k=k: halo_copy(i, k).wait_recv())
        everyone.wait_send()
        for k, (dx, dy) in enumerate(DIRS):
            when(dy, True, lambda k=k: halo_copy(i, k).wait_send())

        def edge_row(at, f, k):
            part = slice(k % 2 * members, (k % 2 + 1) * members)
            return slab[i, at, f, k // 2].astype(F32)[part]

        for f, ref in enumerate((eta, uu, vv)):
            for e in range(ext_tiles):
                joined = jnp.where(lane % (2 * HALO) < HALO, land[i, 0, f, e], land[i, 1, f, e])
                for k in range(BLOCK):
                    r = e * BLOCK + k
                    if e == 0:
                        main = edge_row(0, f, k)
                    elif e == ext_tiles - 1:
                        main = edge_row(1, f, k)
                    else:
                        main = own[f, r - HALO]
                    side = pltpu.roll(joined, (-(2 * HALO * k + HALO)) % cols, 1)
                    if f == 0:
                        main = half * (main - fine[e, :, :cols])
                        side = half * (side - fine[e, :, cols:])
                    if f == 0 or e in (0, ext_tiles - 1):
                        ref[0, r, :, :cols] = main
                    ref[0, r, :, cols:] = side

        for step in range(STEPS):
            sweep(step)
        last = STEPS % 2
        for r in range(rows):
            own[0, r] = eta[last, HALO + r, :, :cols] * (1.0 / half) + fine[1 + r // BLOCK, :, :cols]
            own[1, r] = uu[last, HALO + r, :, :cols]
            own[2, r] = vv[last, HALO + r, :, :cols]
        pl.when(i < INTERVALS - 1)(lambda: begin(i + 1))
        return 0

    begin(0)
    early_setup()
    pl.semaphore_wait(barrier, n - 1)
    for k, (dx, dy) in enumerate(DIRS):
        when(dy, True, lambda k=k: static_copy(k).start())
    lax.fori_loop(0, INTERVALS, interval, 0)


def place_outputs(members, rows, own, l_in, h_out, u_out, v_out, l_out, staged, l_staged, sem):
    copies = [
        pltpu.make_async_copy(staged.at[f], out, sem.at[f]) for f, out in enumerate((h_out, u_out, v_out))
    ]
    for f in range(3):
        for r in range(rows):
            staged[f, pl.ds(r, members, stride=rows), :] = own[f, r]
        copies[f].start()
    blocks, width = l_staged.shape[1:]
    for b in range(blocks):
        l_staged[:, b, :] = l_in[:, b * width : (b + 1) * width]
    copies.append(pltpu.make_async_copy(l_staged, l_out, sem.at[3]))
    copies[3].start()
    for copy in copies:
        copy.wait()


def shards(nx, ny, elevation, east_velocity, north_velocity, water_depth, land_sea):
    members, rows, cols = elevation.shape
    rb_own, cb_own = rows // BLOCK, cols // BLOCK
    n = nx * ny
    ext = rows + 2 * HALO
    tiles = ext // BLOCK
    flat = (members * rows, cols)
    hbm_spec = pl.BlockSpec(memory_space=pltpu.HBM)
    vmem_spec = pl.BlockSpec(memory_space=pltpu.VMEM)
    dma = pltpu.SemaphoreType.DMA
    field = jax.ShapeDtypeStruct(flat, F32)
    own, loading = pl.pallas_call(
        functools.partial(kernel, nx, ny, members, rows, cols),
        out_shape=(
            jax.ShapeDtypeStruct((3, rows, members, cols), F32),
            jax.ShapeDtypeStruct((members, rb_own * cb_own), F32),
        ),
        in_specs=[hbm_spec] * 5,
        out_specs=(vmem_spec,) * 2,
        scratch_shapes=[
            pltpu.VMEM((3,) + flat, F32),
            pltpu.VMEM((rows, cols), F32),
            pltpu.VMEM((rows, cols), jnp.int32),
            pltpu.VMEM((INTERVALS, 3, rb_own, members, cols), F32),
            pltpu.VMEM((INTERVALS, 2, 3, tiles, members, cols), F32),
            pltpu.VMEM((INTERVALS, 2, 3, HALO // 2, 2 * members, cols), BF16),
            pltpu.VMEM((INTERVALS, 2, 3, HALO // 2, 2 * members, cols), BF16),
            pltpu.VMEM((rows, cols), F32),
            pltpu.VMEM((2, ext, cols), F32),
            pltpu.VMEM((2, HALO, cols), F32),
            pltpu.VMEM((ext, members, 2 * cols), F32),
            pltpu.VMEM((ext, members, cols), F32),
            pltpu.VMEM((2, ext, members, 2 * cols), F32),
            pltpu.VMEM((2, ext, members, 2 * cols), F32),
            pltpu.VMEM((2, ext, members, 2 * cols), F32),
            pltpu.VMEM((n // 2, 2 * rb_own * cb_own, 128), BF16),
            pltpu.VMEM((INTERVALS, n, members, 2 * rb_own * cb_own), BF16),
            pltpu.VMEM((tiles, members, 2 * cols), F32),
            pltpu.VMEM((rb_own * cols, 2 * rb_own * cb_own), BF16),
            pltpu.VMEM((128, tiles * 2 * cols), BF16),
            dma((5,)),
            dma((INTERVALS,)),
            dma((INTERVALS,)),
            dma((INTERVALS, len(DIRS))),
            dma((INTERVALS, len(DIRS))),
            dma((len(DIRS),)),
            dma((len(DIRS),)),
        ],
        compiler_params=pltpu.CompilerParams(
            collective_id=0, has_side_effects=True, vmem_limit_bytes=48 * 1024 * 1024
        ),
        name="tide",
    )(
        *(
            pltpu.with_memory_space_constraint(x, pltpu.HBM)
            for x in (
                elevation.reshape(flat), east_velocity.reshape(flat), north_velocity.reshape(flat),
                water_depth, land_sea,
            )
        )
    )
    coarse = jax.ShapeDtypeStruct((members, rb_own, cb_own), F32)
    h, u, v, loading = pl.pallas_call(
        functools.partial(place_outputs, members, rows),
        out_shape=(field, field, field, coarse),
        in_specs=[vmem_spec] * 2,
        out_specs=(hbm_spec,) * 4,
        scratch_shapes=[pltpu.VMEM((3,) + flat, F32), pltpu.VMEM(coarse.shape, F32), dma((4,))],
        compiler_params=pltpu.CompilerParams(vmem_limit_bytes=4 * 1024 * 1024),
        name="place",
    )(own, loading)
    shape = (members, rows, cols)
    return (h.reshape(shape), u.reshape(shape), v.reshape(shape), loading)


def solution(mesh):
    nx, ny = mesh.shape["gx"], mesh.shape["gy"]
    tile = P(None, "gy", "gx")
    return jax.shard_map(
        functools.partial(shards, nx, ny),
        mesh=mesh,
        in_specs=(tile, tile, tile, P("gy", "gx"), P("gy", "gx")),
        out_specs=(tile, tile, tile, tile),
        check_vma=False,
    )
```
